32 devices in a mesh: groups: 2 (over y), tm: 4 (over z), mp: 4 (over x, core).
Axes of the slice: x: 2, y: 2, z: 4, core: 2. Of those that a mesh axis runs over, the one named last changes fastest.
Arguments:
- waveform: float32 [1310720], P(('groups', 'tm', 'mp')), parts along dimension 0, may hold values from -0.8 to 0.8
- segment_start: int32 [2048], P(('groups', 'tm')), parts along dimension 0, may hold values from 0 to 1023, as said below
- segment_end: int32 [2048], P(('groups', 'tm')), parts along dimension 0, may hold values from 1 to 1024, as said below
- w_subsample: bfloat16 [512, 1536], replicated, may hold values from -0.25 to 0.25
- w_attention: bfloat16 [3, 1536, 1536], P(None, None, 'mp')
- w_output: bfloat16 [1536, 1536], P('mp'), may hold values from -0.15625 to 0.15625
- gain_convolution: float32 [1536], replicated, may hold values from 0.1 to 1.9
- w_depthwise: bfloat16 [31, 1536], replicated, may hold values from -1 to 1
Outputs:
- encoded: bfloat16 [2048, 1536], P(('groups', 'tm', 'mp')), parts along dimension 0
The draws below stay inside these ranges and needn't reach their ends.
There are 2 independent parts, one for each index of `groups`. The reference program is written for one: setup_inputs(seed, part) draws one part's arguments, and reference() takes and returns one part's arrays. A program takes and returns all parts, laid end to end along the dimension named above; an argument that names none is the same for every part. Nothing has to cross between parts.
Inputs may be any that keep to these rules, and one draw needn't show every extreme that they name: Segments are contiguous runs of frames that tile the slab: segment_start[i] <= i < segment_end[i], and all frames of a run share both values; every run has 150 to 750 frames except the first and the last, which may be shorter; one run of exactly 750 frames lies in every draw. `segment_end`: the end of the run holding each frame, as described for segment_start.
All inputs are finite; a program needn't handle non-finite values.
Results may differ from the reference program's by a relative error of at most 0.015.
Values may be sent and summed in bfloat16 or wider, within the bound.
A program may use at most 64 MiB of HBM per device.

```python
import math
import jax
import jax.numpy as jnp
from jax import lax

D = 1536
HEADS = 24
HD = 64
NMEL = 128
NFFT = 400
HOP = 160
BINS = 256
SUB = 4
KERNEL = 31
SEG_MAX = 750
FT = 256
FRAMES = 1024
SAMPLES = 655360
N_MP = 4


def segment_bounds(key):
    shortest = SEG_MAX // 5
    run_count = FRAMES // shortest + 2
    offset = jax.random.randint(jax.random.fold_in(key, 12), (), 0, FRAMES - SEG_MAX + 1, dtype=jnp.int32)
    left_lengths = jax.random.randint(jax.random.fold_in(key, 11), (run_count,), shortest, SEG_MAX + 1, dtype=jnp.int32)
    right_lengths = jax.random.randint(jax.random.fold_in(key, 13), (run_count,), shortest, SEG_MAX + 1, dtype=jnp.int32)
    left_bounds = jnp.maximum(offset - jnp.cumsum(left_lengths).astype(jnp.int32), 0)
    right_bounds = jnp.minimum(offset + SEG_MAX + jnp.cumsum(right_lengths).astype(jnp.int32), FRAMES)
    fixed_bounds = jnp.stack([jnp.zeros((), jnp.int32), offset, offset + SEG_MAX, jnp.full((), FRAMES, jnp.int32)]).astype(jnp.int32)
    bounds = jnp.concatenate([fixed_bounds, left_bounds, right_bounds]).astype(jnp.int32)
    frame_index = jnp.arange(FRAMES, dtype=jnp.int32)
    starts = jnp.max(jnp.where(bounds[None, :] <= frame_index[:, None], bounds[None, :], 0), axis=1).astype(jnp.int32)
    finish = jnp.min(jnp.where(bounds[None, :] > frame_index[:, None], bounds[None, :], FRAMES), axis=1).astype(jnp.int32)
    return (starts, finish)


def draw_segment_start(key, part):
    return segment_bounds(jax.random.fold_in(key, 5))[0]


def draw_segment_end(key, part):
    return segment_bounds(jax.random.fold_in(key, 5))[1]


def draw_w_attention(key, part):
    base = jax.random.normal(jax.random.fold_in(key, 1), (3, D, D), jnp.float32) / math.sqrt(D)
    value_part = base[2] * 3.0
    return jnp.stack([base[0], base[1], value_part]).astype(jnp.bfloat16)


def shard_levels(own_key, shape, cuts, low, largest):
    def one(dim, parts):
        steps = jax.random.uniform(jax.random.fold_in(jax.random.fold_in(own_key, 6), dim), (parts,), jnp.float32, low / len(cuts), largest / len(cuts))
        return jnp.repeat(jnp.exp(steps), shape[dim] // parts).reshape((-1,) + (1,) * (len(shape) - dim - 1))

    gain = one(*cuts[0])
    for cut in cuts[1:]:
        gain = gain * one(*cut)
    return gain


def centred(stream_key, dims, width, reach, cuts=(), held_as=jnp.bfloat16):
    gain = shard_levels(stream_key, dims, cuts, -0.22, 0.18) if cuts else 1.0
    drawn = jax.random.normal(stream_key, dims, jnp.float32) * width * gain
    return jnp.minimum(jnp.maximum(drawn, -reach), reach).astype(held_as)


def setup_inputs(seed: int = 0, part: int = 0) -> dict:
    seeds = jax.random.split(jax.random.key(seed), 9)
    part_keys = jax.random.split(jax.random.fold_in(seeds[8], part), 9)
    return {
        "waveform": centred(part_keys[0], (SAMPLES,), 0.1, 0.8, ((0, 16),), jnp.float32),
        "segment_start": draw_segment_start(jax.random.fold_in(jax.random.fold_in(seeds[8], part), 71), part),
        "segment_end": draw_segment_end(jax.random.fold_in(jax.random.fold_in(seeds[8], part), 71), part),
        "w_subsample": centred(seeds[3], (SUB * NMEL, D), (SUB * NMEL) ** -0.5, 0.25),
        "w_attention": draw_w_attention(jax.random.fold_in(seeds[8], 71), part),
        "w_output": centred(seeds[5], (D, D), D ** -0.5, 0.15625, ((0, 4),)),
        "gain_convolution": jnp.clip(1.0 + 0.18 * jax.random.normal(seeds[6], (D,), jnp.float32), 0.1, 1.9),
        "w_depthwise": centred(seeds[7], (KERNEL, D), KERNEL ** -0.5, 1.0),
    }


def fourier_table():
    sample_index = jnp.arange(NFFT, dtype=jnp.int32)[:, None]
    bin_index = jnp.arange(BINS, dtype=jnp.int32)[None, :]
    phase_int = sample_index * bin_index % NFFT
    angle_rad = phase_int.astype(jnp.float32) * (2.0 * math.pi / NFFT)
    window_row = 0.5 - 0.5 * jnp.cos(jnp.arange(NFFT, dtype=jnp.float32) * (2.0 * math.pi / NFFT))
    kept_bins = bin_index <= NFFT // 2
    cosine_part = jnp.where(kept_bins, jnp.cos(angle_rad), 0.0) * window_row[:, None]
    sine_part = jnp.where(kept_bins, -jnp.sin(angle_rad), 0.0) * window_row[:, None]
    return jnp.concatenate([cosine_part, sine_part], axis=1)

def mel_bank():
    mel_top = 2595.0 * math.log10(1.0 + 8000.0 / 700.0)
    mel_points = jnp.arange(NMEL + 2, dtype=jnp.float32) * (mel_top / (NMEL + 1))
    hertz_points = 700.0 * (jnp.power(10.0, mel_points / 2595.0) - 1.0)
    edges = hertz_points * (NFFT / 16000.0)
    centers = edges[1:-1]
    widths = jnp.maximum(edges[2:] - edges[1:-1], 1.0)
    bin_value = jnp.arange(BINS, dtype=jnp.float32)[:, None]
    triangle = jnp.maximum(0.0, 1.0 - jnp.abs(bin_value - centers[None, :]) / widths[None, :])
    return jnp.where(bin_value <= NFFT // 2, triangle, 0.0)

def frame_rows(padded, frame_count):
    blocks_needed = -(-NFFT // HOP)
    blocks = padded[:(frame_count + blocks_needed - 1) * HOP].reshape(frame_count + blocks_needed - 1, HOP)
    pieces = [blocks[offset:offset + frame_count] for offset in range(blocks_needed)]
    return jnp.concatenate(pieces, axis=1)[:, :NFFT]

def log_mel(frames):
    spectrum = jnp.dot(frames, fourier_table(), precision=lax.Precision.HIGHEST, preferred_element_type=jnp.float32)
    spectral_power = jnp.square(spectrum[:, :BINS]) + jnp.square(spectrum[:, BINS:])
    energy = jnp.dot(spectral_power, mel_bank(), precision=lax.Precision.HIGHEST, preferred_element_type=jnp.float32)
    return jnp.log(energy + 1e-06)

def normalize(values):
    values = values.astype(jnp.float32)
    center = lax.optimization_barrier(jnp.mean(values, axis=-1, keepdims=True))
    spread = lax.optimization_barrier(jnp.mean(jnp.square(values - center), axis=-1, keepdims=True))
    return (values - center) * lax.rsqrt(spread + 1e-05)

def layer_norm(values, gain_row):
    return normalize(values) * gain_row.astype(jnp.float32)

def reference(waveform, segment_start, segment_end, w_subsample, w_attention, w_output, gain_convolution, w_depthwise):
    blocks_needed = -(-NFFT // HOP)
    padded = jnp.concatenate([waveform, jnp.zeros((blocks_needed * HOP,), waveform.dtype)])
    stacked = log_mel(frame_rows(padded, FRAMES * SUB)).reshape(FRAMES, SUB * NMEL).astype(jnp.bfloat16)
    features = lax.optimization_barrier(jnp.dot(stacked, w_subsample, preferred_element_type=jnp.float32).astype(jnp.bfloat16))
    normed = normalize(features).astype(jnp.bfloat16)
    queries = lax.optimization_barrier(jnp.dot(normed, w_attention[0], preferred_element_type=jnp.float32).astype(jnp.bfloat16))
    key_rows = lax.optimization_barrier(jnp.dot(normed, w_attention[1], preferred_element_type=jnp.float32).astype(jnp.bfloat16))
    value_rows = lax.optimization_barrier(jnp.dot(normed, w_attention[2], preferred_element_type=jnp.float32).astype(jnp.bfloat16))
    key_pad = jnp.pad(key_rows, ((SEG_MAX, SEG_MAX), (0, 0)))
    value_pad = jnp.pad(value_rows, ((SEG_MAX, SEG_MAX), (0, 0)))
    scale_factor = 1.0 / math.sqrt(HD)
    window_len = FT + 2 * SEG_MAX

    def attend_block(block_index):
        begin_row = block_index * FT
        query_block = lax.dynamic_slice_in_dim(queries, begin_row, FT, 0).astype(jnp.float32).reshape(FT, HEADS, HD)
        key_block = lax.dynamic_slice_in_dim(key_pad, begin_row, window_len, 0).astype(jnp.float32).reshape(window_len, HEADS, HD)
        value_block = lax.dynamic_slice_in_dim(value_pad, begin_row, window_len, 0).astype(jnp.float32).reshape(window_len, HEADS, HD)
        positions = begin_row - SEG_MAX + jnp.arange(window_len, dtype=jnp.int32)
        starts = lax.dynamic_slice_in_dim(segment_start, begin_row, FT, 0)
        finish = lax.dynamic_slice_in_dim(segment_end, begin_row, FT, 0)
        scores = jnp.einsum('qhd,khd->qhk', query_block, key_block) * scale_factor
        allowed = (positions[None, :] >= starts[:, None]) & (positions[None, :] < finish[:, None])
        scores = jnp.where(allowed[:, None, :], scores, -1e+30)
        row_max = lax.optimization_barrier(jnp.max(scores, axis=-1, keepdims=True))
        weights = jnp.exp(scores - row_max)
        rounded = lax.optimization_barrier(weights.astype(jnp.bfloat16)).astype(jnp.float32)
        numerator = jnp.einsum('qhk,khd->qhd', rounded, value_block)
        denominator = lax.optimization_barrier(jnp.sum(weights, axis=-1))
        return (numerator / denominator[..., None]).reshape(FT, D).astype(jnp.bfloat16)
    attended = lax.map(attend_block, jnp.arange(FRAMES // FT, dtype=jnp.int32)).reshape(FRAMES, D)
    group_width = D // N_MP
    branch = jnp.zeros((FRAMES, D), jnp.float32)
    for group_index in range(N_MP):
        lower = group_index * group_width
        partial_sum = jnp.dot(attended[:, lower:lower + group_width], w_output[lower:lower + group_width], preferred_element_type=jnp.float32)
        branch = branch + lax.optimization_barrier(partial_sum.astype(jnp.bfloat16)).astype(jnp.float32)
    mixed_rows = lax.optimization_barrier((features.astype(jnp.float32) + branch).astype(jnp.bfloat16))
    conv_input = lax.optimization_barrier(layer_norm(mixed_rows, gain_convolution).astype(jnp.bfloat16))
    half_kernel = KERNEL // 2
    padded_conv = jnp.pad(conv_input.astype(jnp.float32), ((half_kernel, half_kernel), (0, 0)))
    convolved = jnp.zeros((FRAMES, D), jnp.float32)
    for tap_index in range(KERNEL):
        convolved = convolved + padded_conv[tap_index:tap_index + FRAMES] * w_depthwise[tap_index].astype(jnp.float32)
    return (mixed_rows.astype(jnp.float32) + jax.nn.silu(convolved)).astype(jnp.bfloat16)
```

```python
import functools
import math

import jax
import jax.numpy as jnp
import numpy as np
from jax import lax
from jax.experimental import pallas as pl
from jax.experimental.pallas import tpu as pltpu
from jax.sharding import PartitionSpec as P

HD = 64
NMEL = 128
NFFT = 400
HOP = 160
BINS = 256
SUB = 4
KERNEL = 31
SEG_MAX = 750
LANES = 128
WIN = 512
EDGE = 16
MESH = pl.DeviceIdType.MESH
F32 = jnp.float32
BF16 = jnp.bfloat16


def fourier_table():
    sample_index = np.arange(NFFT)[:, None]
    bin_index = np.arange(BINS)[None, :]
    angle = (sample_index * bin_index % NFFT) * (2.0 * math.pi / NFFT)
    window = 0.5 - 0.5 * np.cos(np.arange(NFFT) * (2.0 * math.pi / NFFT))
    kept = bin_index <= NFFT // 2
    cosine = np.where(kept, np.cos(angle), 0.0) * window[:, None]
    sine = np.where(kept, -np.sin(angle), 0.0) * window[:, None]
    table = np.concatenate([cosine, sine], axis=1)
    return np.concatenate([table, np.zeros((WIN - NFFT, 2 * BINS))], axis=0)


def mel_bank():
    mel_top = 2595.0 * math.log10(1.0 + 8000.0 / 700.0)
    points = np.arange(NMEL + 2) * (mel_top / (NMEL + 1))
    edges = 700.0 * (np.power(10.0, points / 2595.0) - 1.0) * (NFFT / 16000.0)
    centers = edges[1:-1]
    widths = np.maximum(edges[2:] - edges[1:-1], 1.0)
    bins = np.arange(BINS)[:, None]
    triangle = np.maximum(0.0, 1.0 - np.abs(bins - centers[None, :]) / widths[None, :])
    return np.where(bins <= NFFT // 2, triangle, 0.0)


def halves(values):
    values = values.astype(np.float32)
    high = values.astype(BF16)
    low = (values - high.astype(np.float32)).astype(BF16)
    return np.stack([high, low])


def split(values):
    high = values.astype(BF16)
    return high, (values - high.astype(F32)).astype(BF16)


def wide_dot(values, table):
    high, low = split(values)
    dot = functools.partial(jnp.dot, preferred_element_type=F32)
    return dot(high, table[0]) + (dot(high, table[1]) + dot(low, table[0]))


def flipped(index, bit):
    return index + bit - 2 * bit * ((index // bit) % 2)


def masked_index(index, mask):
    bit = 1
    while bit <= mask:
        if mask & bit:
            index = flipped(index, bit)
        bit *= 2
    return index


def bits_of(count):
    bits = []
    bit = 1
    while bit < count:
        bits.append(bit)
        bit *= 2
    return bits


def low_bit(mask, count):
    return mask & -mask if mask else count


def normalize(values):
    center = jnp.mean(values, axis=-1, keepdims=True)
    shifted = values - center
    spread = jnp.mean(jnp.square(shifted), axis=-1, keepdims=True)
    return shifted * lax.rsqrt(spread + 1e-05)


def beside(t, m, n_t, n_m, step):
    flat = t * n_m + m + step
    return {"tm": flat // n_m, "mp": flat % n_m}


def signal(sem, device):
    pl.semaphore_signal(sem, inc=1, device_id=device, device_id_type=MESH)


def front_kernel(
    n_t, n_m, reach, absolute, audio_ref, table_ref, bank_ref, out_ref,
    rows, edge_sem, tm_send, mp_send, recv,
):
    t = lax.axis_index("tm")
    m = lax.axis_index("mp")
    own = out_ref.shape[2]
    stride = SUB * HOP // LANES
    flat = t * n_m + m
    has_prev = flat > 0
    has_next = flat < n_t * n_m - 1
    bits = bits_of(n_m)
    distances = []
    for d in range(1, reach + 1):
        distances += [d, -d]
    rows[pl.ds(0, own * stride), :] = audio_ref[...]
    rows[pl.ds(own * stride, 8), :] = jnp.zeros((8, LANES), F32)
    if not absolute:
        out_ref[...] = jnp.zeros_like(out_ref)

    barrier = pltpu.get_barrier_semaphore()

    def slot_of(distance):
        return t - distance if absolute else reach - distance

    for d in distances:
        inside = jnp.logical_and(t + d >= 0, t + d < n_t)

        @pl.when(inside)
        def _(d=d):
            signal(barrier, {"tm": t + d, "mp": m})

    for bit in bits:
        signal(barrier, {"tm": t, "mp": flipped(m, bit)})

    @pl.when(has_prev)
    def _():
        signal(barrier, beside(t, m, n_t, n_m, -1))

    @pl.when(has_next)
    def _():
        signal(barrier, beside(t, m, n_t, n_m, 1))

    peers = len(bits) + has_prev.astype(jnp.int32) + has_next.astype(jnp.int32)
    for d in distances:
        peers = peers + jnp.logical_and(t + d >= 0, t + d < n_t).astype(jnp.int32)
    pl.semaphore_wait(barrier, peers)

    def head_copy(device):
        return pltpu.make_async_remote_copy(
            src_ref=audio_ref.at[pl.ds(0, 8)],
            dst_ref=rows.at[pl.ds(own * stride, 8)],
            send_sem=edge_sem.at[0],
            recv_sem=edge_sem.at[1],
            device_id=device,
            device_id_type=MESH,
        )

    @pl.when(has_prev)
    def _():
        head_copy(beside(t, m, n_t, n_m, -1)).start()

    @pl.when(has_next)
    def _():
        head_copy(beside(t, m, n_t, n_m, 1)).wait_recv()

    pieces = [rows[pl.ds(j, own, stride=stride), :] for j in range(stride + 2)]
    frames = []
    for j in range(SUB):
        window = jnp.concatenate(pieces[j : j + WIN // LANES], axis=1)
        shift = (HOP - LANES) * j
        frames.append(pltpu.roll(window, WIN - shift, 1) if shift else window)
    spectrum = wide_dot(jnp.concatenate(frames, axis=0), table_ref)
    power = jnp.square(spectrum[:, :BINS]) + jnp.square(spectrum[:, BINS:])
    mel = jnp.log(wide_dot(power, bank_ref) + 1e-06).astype(BF16)
    here = slot_of(0)
    for j in range(SUB):
        out_ref[here, m, :, pl.ds(NMEL * j, NMEL)] = mel[j * own : (j + 1) * own]

    def tm_copy(d, slot, device):
        return pltpu.make_async_remote_copy(
            src_ref=out_ref.at[here, m],
            dst_ref=out_ref.at[slot, m],
            send_sem=tm_send.at[d + reach],
            recv_sem=recv.at[d + reach, 0],
            device_id=device,
            device_id_type=MESH,
        )

    def mp_copy(d, mask, bit):
        block = out_ref.at[slot_of(d), masked_index(m, mask)]
        return pltpu.make_async_remote_copy(
            src_ref=block,
            dst_ref=block,
            send_sem=mp_send.at[d + reach, mask + bit],
            recv_sem=recv.at[d + reach, mask + bit],
            device_id={"tm": t, "mp": flipped(m, bit)},
            device_id_type=MESH,
        )

    def forward(d, mask):
        for bit in reversed(bits):
            if bit < low_bit(mask, n_m):
                mp_copy(d, mask, bit).start()

    for d in distances:

        @pl.when(jnp.logical_and(t + d >= 0, t + d < n_t))
        def _(d=d):
            landing = t if absolute else reach - d
            tm_copy(d, landing, {"tm": t + d, "mp": m}).start()

    forward(0, 0)
    order = [0] + distances

    def when_held(d, body):
        if d == 0:
            body()
        else:
            pl.when(jnp.logical_and(t - d >= 0, t - d < n_t))(body)

    masks = sorted(range(1, n_m), key=lambda v: -low_bit(v, n_m))
    for d in distances:

        def arrive(d=d):
            landing = t if absolute else reach - d
            tm_copy(d, landing, {"tm": t, "mp": m}).wait_recv()
            forward(d, 0)

        when_held(d, arrive)
    for mask in masks:
        bit = low_bit(mask, n_m)
        for d in order:

            def relay(d=d, mask=mask, bit=bit):
                mp_copy(d, mask - bit, bit).wait_recv()
                forward(d, mask)

            when_held(d, relay)
    for d in distances:

        @pl.when(jnp.logical_and(t + d >= 0, t + d < n_t))
        def _(d=d):
            landing = t if absolute else reach - d
            tm_copy(d, landing, {"tm": t + d, "mp": m}).wait_send()

    for mask in range(1, n_m):
        bit = low_bit(mask, n_m)
        for d in order:

            def drain(d=d, mask=mask, bit=bit):
                mp_copy(d, mask - bit, bit).wait_send()

            when_held(d, drain)

    @pl.when(has_prev)
    def _():
        head_copy(beside(t, m, n_t, n_m, -1)).wait_send()


def heads_kernel(
    n_t, n_m, reach, absolute, place_ref, stacked_ref, start_ref, finish_ref, wsub_ref, watt_ref,
    wout_ref, part_ref, own_ref, feats, query, keys, values, attended,
):
    t = place_ref[0]
    m = place_ref[1]
    slots = stacked_ref.shape[0]
    own = stacked_ref.shape[2]
    shard = n_m * own
    width = watt_ref.shape[2]
    heads = width // HD
    mine = t if absolute else reach
    dot = functools.partial(jnp.dot, preferred_element_type=F32)
    for slot in range(slots):
        block = stacked_ref[slot].reshape(shard, SUB * NMEL)
        features = dot(block, wsub_ref[...]).astype(BF16)
        feats[pl.ds(slot * shard, shard), :] = features
        normed = normalize(features.astype(F32)).astype(BF16)
        keys[pl.ds(slot * shard, shard), :] = dot(normed, watt_ref[1]).astype(BF16)
        values[pl.ds(slot * shard, shard), :] = dot(normed, watt_ref[2]).astype(BF16)

        @pl.when(mine == slot)
        def _(normed=normed):
            asked = dot(normed, watt_ref[0]).astype(BF16)
            query[...] = (asked.astype(F32) * (1.0 / math.sqrt(HD))).astype(BF16)

    own_row = pl.multiple_of(mine * shard + m * own, own)
    own_ref[...] = feats[pl.ds(own_row, own), :]
    count = slots * shard
    begin = 0 if absolute else (t - reach) * shard
    position = lax.broadcasted_iota(jnp.int32, (shard, count), 1) + begin

    def column(ref):
        wide = jnp.broadcast_to(ref[...].astype(F32), (LANES, shard))
        return jnp.transpose(wide)[:, :1].astype(jnp.int32)

    allowed = jnp.logical_and(position >= column(start_ref), position < column(finish_ref))
    for head in range(heads):
        cut = slice(head * HD, (head + 1) * HD)
        scores = lax.dot_general(
            query[:, cut], keys[:, cut], (((1,), (1,)), ((), ())), preferred_element_type=F32
        )
        scores = jnp.where(allowed, scores, -1e30)
        weights = jnp.exp(scores - jnp.max(scores, axis=-1, keepdims=True))
        total = jnp.sum(weights, axis=-1, keepdims=True)
        attended[:, cut] = (dot(weights.astype(BF16), values[:, cut]) / total).astype(BF16)
    part_ref[...] = dot(attended[...], wout_ref[...]).astype(BF16)


def tail_kernel(
    n_t, n_m, part_ref, feature_ref, gain_ref, taps_ref, out_ref,
    landed, outgoing, mixed, edges, padded, part_send, part_recv, edge_send, edge_recv,
):
    t = lax.axis_index("tm")
    m = lax.axis_index("mp")
    own, width = feature_ref.shape
    flat = t * n_m + m
    has_prev = flat > 0
    has_next = flat < n_t * n_m - 1
    bits = bits_of(n_m)
    barrier = pltpu.get_barrier_semaphore()
    for bit in bits:
        signal(barrier, {"tm": t, "mp": flipped(m, bit)})

    @pl.when(has_prev)
    def _():
        signal(barrier, beside(t, m, n_t, n_m, -1))

    @pl.when(has_next)
    def _():
        signal(barrier, beside(t, m, n_t, n_m, 1))

    peers = len(bits) + has_prev.astype(jnp.int32) + has_next.astype(jnp.int32)
    pl.semaphore_wait(barrier, peers)

    def part_rows(mask):
        return pl.ds(pl.multiple_of(masked_index(m, mask) * own, own), own)

    slot_index = {}
    for bit in bits:
        for mask in range(n_m):
            if mask % (2 * bit) == 0:
                slot_index[bit, mask] = len(slot_index)

    def part_copy(bit, mask):
        index = slot_index[bit, mask]
        source = part_ref.at[part_rows(mask + bit)] if bit == 1 else outgoing.at[mask + bit]
        return pltpu.make_async_remote_copy(
            src_ref=source,
            dst_ref=landed.at[index],
            send_sem=part_send.at[index],
            recv_sem=part_recv.at[index],
            device_id={"tm": t, "mp": flipped(m, bit)},
            device_id_type=MESH,
        )

    total = {}
    for bit in bits:
        kept = [mask for mask in range(n_m) if mask % (2 * bit) == 0]
        kept = kept[::-1]
        if bit == 1:
            for mask in kept:
                part_copy(bit, mask).start()
        for mask in kept:
            part_copy(bit, mask).wait_recv()
            if bit == 1:
                base = part_ref[part_rows(mask), :].astype(F32)
            else:
                base = total[mask]
            total[mask] = base + landed[slot_index[bit, mask]].astype(F32)
            after = 2 * bit
            if mask % (2 * after) == after and after < n_m:
                outgoing[mask] = total[mask].astype(BF16)
                part_copy(after, mask - after).start()
    branch = total[0] if total else part_ref[...].astype(F32)
    blended = (feature_ref[...].astype(F32) + branch).astype(BF16)
    mixed[...] = blended
    normed = (normalize(blended.astype(F32)) * gain_ref[...]).astype(BF16)
    edges[0] = normed[:EDGE]
    edges[1] = normed[own - EDGE :]

    def edge_copy(side):
        return pltpu.make_async_remote_copy(
            src_ref=edges.at[side],
            dst_ref=edges.at[2 + side],
            send_sem=edge_send.at[side],
            recv_sem=edge_recv.at[side],
            device_id=beside(t, m, n_t, n_m, 2 * side - 1),
            device_id_type=MESH,
        )

    @pl.when(has_prev)
    def _():
        edge_copy(0).start()

    @pl.when(has_next)
    def _():
        edge_copy(1).start()

    padded[pl.ds(EDGE, own), :] = normed.astype(F32)
    padded[pl.ds(0, EDGE), :] = jnp.zeros((EDGE, width), F32)
    padded[pl.ds(EDGE + own, EDGE), :] = jnp.zeros((EDGE, width), F32)

    @pl.when(has_next)
    def _():
        edge_copy(0).wait_recv()
        padded[pl.ds(EDGE + own, EDGE), :] = edges[2].astype(F32)

    @pl.when(has_prev)
    def _():
        edge_copy(1).wait_recv()
        padded[pl.ds(0, EDGE), :] = edges[3].astype(F32)

    offset = EDGE - KERNEL // 2

    @pl.loop(0, width // LANES)
    def _(chunk):
        cols = pl.ds(pl.multiple_of(chunk * LANES, LANES), LANES)
        taps = taps_ref[:, cols].astype(F32)
        convolved = jnp.zeros((own, LANES), F32)
        for tap in range(KERNEL):
            convolved = convolved + padded[pl.ds(offset + tap, own), cols] * taps[tap : tap + 1]
        gated = convolved / (1.0 + jnp.exp(-convolved))
        out_ref[:, cols] = (mixed[:, cols].astype(F32) + gated).astype(BF16)

    for bit in bits:
        for mask in range(n_m):
            if mask % (2 * bit) == 0:
                part_copy(bit, mask).wait_send()

    @pl.when(has_prev)
    def _():
        edge_copy(0).wait_send()

    @pl.when(has_next)
    def _():
        edge_copy(1).wait_send()


VMEM = pl.BlockSpec(memory_space=pltpu.VMEM)
SMEM = pl.BlockSpec(memory_space=pltpu.SMEM)


def shards(
    n_t, n_m, waveform, segment_start, segment_end, w_subsample, w_attention, w_output,
    gain_convolution, w_depthwise,
):
    own = waveform.shape[0] // (SUB * HOP)
    shard = segment_start.shape[0]
    stacked_width, width = w_subsample.shape
    local = w_attention.shape[2]
    reach = min((SEG_MAX - 2) // shard + 1, n_t - 1)
    absolute = 2 * reach + 1 >= n_t
    slots = n_t if absolute else 2 * reach + 1
    lines = own * SUB * HOP // LANES
    audio = waveform.reshape(lines, LANES)
    dma = pltpu.SemaphoreType.DMA
    stacked = pl.pallas_call(
        functools.partial(front_kernel, n_t, n_m, reach, absolute),
        out_shape=jax.ShapeDtypeStruct((slots, n_m, own, stacked_width), BF16),
        in_specs=[VMEM] * 3,
        out_specs=VMEM,
        scratch_shapes=[
            pltpu.VMEM((lines + 8, LANES), F32),
            dma((2,)),
            dma((2 * reach + 1,)),
            dma((2 * reach + 1, n_m)),
            dma((2 * reach + 1, n_m)),
        ],
        compiler_params=pltpu.CompilerParams(collective_id=0, has_side_effects=True),
        name="front",
    )(audio, jnp.asarray(halves(fourier_table())), jnp.asarray(halves(mel_bank())))
    place = jnp.stack([lax.axis_index("tm"), lax.axis_index("mp")]).astype(jnp.int32)
    part, features = pl.pallas_call(
        functools.partial(heads_kernel, n_t, n_m, reach, absolute),
        out_shape=(
            jax.ShapeDtypeStruct((shard, width), BF16),
            jax.ShapeDtypeStruct((own, width), BF16),
        ),
        in_specs=[SMEM] + [VMEM] * 6,
        out_specs=(VMEM, VMEM),
        scratch_shapes=[
            pltpu.VMEM((slots * shard, width), BF16),
            pltpu.VMEM((shard, local), BF16),
            pltpu.VMEM((slots * shard, local), BF16),
            pltpu.VMEM((slots * shard, local), BF16),
            pltpu.VMEM((shard, local), BF16),
        ],
        name="heads",
    )(
        place, stacked, segment_start.reshape(1, shard), segment_end.reshape(1, shard),
        w_subsample, w_attention, w_output,
    )
    landings = max(n_m - 1, 1)
    return pl.pallas_call(
        functools.partial(tail_kernel, n_t, n_m),
        out_shape=jax.ShapeDtypeStruct((own, width), BF16),
        in_specs=[VMEM] * 4,
        out_specs=VMEM,
        scratch_shapes=[
            pltpu.VMEM((landings, own, width), BF16),
            pltpu.VMEM((n_m, own, width), BF16),
            pltpu.VMEM((own, width), BF16),
            pltpu.VMEM((4, EDGE, width), BF16),
            pltpu.VMEM((own + 2 * EDGE, width), F32),
            dma((landings,)),
            dma((landings,)),
            dma((2,)),
            dma((2,)),
        ],
        compiler_params=pltpu.CompilerParams(collective_id=1, has_side_effects=True),
        name="tail",
    )(part, features, gain_convolution.reshape(1, width), w_depthwise)


def solution(mesh):
    placed = (
        P(("groups", "tm", "mp")),
        P(("groups", "tm")),
        P(("groups", "tm")),
        P(),
        P(None, None, "mp"),
        P("mp", None),
        P(),
        P(),
    )
    return jax.shard_map(
        functools.partial(shards, mesh.shape["tm"], mesh.shape["mp"]),
        mesh=mesh,
        in_specs=placed,
        out_specs=P(("groups", "tm", "mp"), None),
        check_vma=False,
    )
```

```python
import functools
import math

import jax
import jax.numpy as jnp
import numpy as np
from jax import lax
from jax.experimental import pallas as pl
from jax.experimental.pallas import tpu as pltpu
from jax.sharding import PartitionSpec as P

HD = 64
NMEL = 128
NFFT = 400
HOP = 160
BINS = 256
SUB = 4
KERNEL = 31
SEG_MAX = 750
LANES = 128
WIN = 512
EDGE = 16
MESH = pl.DeviceIdType.MESH
F32 = jnp.float32
BF16 = jnp.bfloat16


def fourier_table():
    sample_index = np.arange(NFFT)[:, None]
    bin_index = np.arange(BINS)[None, :]
    angle = (sample_index * bin_index % NFFT) * (2.0 * math.pi / NFFT)
    window = 0.5 - 0.5 * np.cos(np.arange(NFFT) * (2.0 * math.pi / NFFT))
    kept = bin_index <= NFFT // 2
    cosine = np.where(kept, np.cos(angle), 0.0) * window[:, None]
    sine = np.where(kept, -np.sin(angle), 0.0) * window[:, None]
    table = np.concatenate([cosine, sine], axis=1)
    return np.concatenate([table, np.zeros((WIN - NFFT, 2 * BINS))], axis=0)


def mel_bank():
    mel_top = 2595.0 * math.log10(1.0 + 8000.0 / 700.0)
    points = np.arange(NMEL + 2) * (mel_top / (NMEL + 1))
    edges = 700.0 * (np.power(10.0, points / 2595.0) - 1.0) * (NFFT / 16000.0)
    centers = edges[1:-1]
    widths = np.maximum(edges[2:] - edges[1:-1], 1.0)
    bins = np.arange(BINS)[:, None]
    triangle = np.maximum(0.0, 1.0 - np.abs(bins - centers[None, :]) / widths[None, :])
    return np.where(bins <= NFFT // 2, triangle, 0.0)


def halves(values):
    values = values.astype(np.float32)
    high = values.astype(BF16)
    low = (values - high.astype(np.float32)).astype(BF16)
    return np.stack([high, low])


def split(values):
    high = values.astype(BF16)
    return high, (values - high.astype(F32)).astype(BF16)


def wide_dot(values, table):
    high, low = split(values)
    dot = functools.partial(jnp.dot, preferred_element_type=F32)
    return dot(high, table[0]) + (dot(high, table[1]) + dot(low, table[0]))


def flipped(index, bit):
    return index + bit - 2 * bit * ((index // bit) % 2)


def masked_index(index, mask):
    bit = 1
    while bit <= mask:
        if mask & bit:
            index = flipped(index, bit)
        bit *= 2
    return index


def bits_of(count):
    bits = []
    bit = 1
    while bit < count:
        bits.append(bit)
        bit *= 2
    return bits


def low_bit(mask, count):
    return mask & -mask if mask else count


def normalize(values):
    center = jnp.mean(values, axis=-1, keepdims=True)
    shifted = values - center
    spread = jnp.mean(jnp.square(shifted), axis=-1, keepdims=True)
    return shifted * lax.rsqrt(spread + 1e-05)


def beside(t, m, n_t, n_m, step):
    flat = t * n_m + m + step
    return {"tm": flat // n_m, "mp": flat % n_m}


def signal(sem, device):
    pl.semaphore_signal(sem, inc=1, device_id=device, device_id_type=MESH)


def block_kernel(
    n_t, n_m, reach, absolute, audio_ref, table_ref, bank_ref, start_ref, finish_ref, gain_ref, taps_ref,
    wsub_hbm, watt_hbm, wout_hbm, out_ref,
    rows, gathered, wsub, watt, wout, folded, query, keys, values, bounds, features, parts, landed, outgoing,
    edges, padded, load_sem, head_sem, tm_send, mp_send, recv, part_send, part_recv, edge_send, edge_recv,
):
    t = lax.axis_index("tm")
    m = lax.axis_index("mp")
    slots, _, own, stacked_width = gathered.shape
    shard = n_m * own
    width = out_ref.shape[1]
    local = watt.shape[2]
    count = slots * shard
    stride = SUB * HOP // LANES
    flat = t * n_m + m
    has_prev = flat > 0
    has_next = flat < n_t * n_m - 1
    bits = bits_of(n_m)
    distances = []
    for d in range(1, reach + 1):
        distances += [d, -d]
    dot = functools.partial(jnp.dot, preferred_element_type=F32)
    here = t if absolute else reach
    prev_device = beside(t, m, n_t, n_m, -1)
    next_device = beside(t, m, n_t, n_m, 1)

    loads = [pltpu.make_async_copy(wsub_hbm, wsub.at[pl.ds(0, stacked_width)], load_sem.at[0])]
    for k in range(3):
        loads.append(pltpu.make_async_copy(watt_hbm.at[k], watt.at[k], load_sem.at[1 + k]))
    loads.append(pltpu.make_async_copy(wout_hbm, wout, load_sem.at[4]))
    for load in loads:
        load.start()

    rows[pl.ds(0, own * stride), :] = audio_ref[...]
    rows[pl.ds(own * stride, 8), :] = jnp.zeros((8, LANES), F32)
    if not absolute:
        gathered[...] = jnp.zeros_like(gathered)
    barrier = pltpu.get_barrier_semaphore()
    peers = len(bits) + has_prev.astype(jnp.int32) + has_next.astype(jnp.int32)
    for d in distances:
        inside = jnp.logical_and(t + d >= 0, t + d < n_t)
        peers = peers + inside.astype(jnp.int32)

        @pl.when(inside)
        def _(d=d):
            signal(barrier, {"tm": t + d, "mp": m})

    for bit in bits:
        signal(barrier, {"tm": t, "mp": flipped(m, bit)})

    @pl.when(has_prev)
    def _():
        signal(barrier, prev_device)

    @pl.when(has_next)
    def _():
        signal(barrier, next_device)

    for index, ref in enumerate((start_ref, finish_ref)):
        wide = jnp.broadcast_to(ref[...].astype(F32), (LANES, shard))
        bounds[index] = jnp.transpose(wide).astype(jnp.int32)
    wsub[pl.ds(stacked_width, EDGE), :] = jnp.ones((EDGE, width), BF16)
    pl.semaphore_wait(barrier, peers)

    def head_copy(device):
        return pltpu.make_async_remote_copy(
            src_ref=audio_ref.at[pl.ds(0, 8)],
            dst_ref=rows.at[pl.ds(own * stride, 8)],
            send_sem=head_sem.at[0],
            recv_sem=head_sem.at[1],
            device_id=device,
            device_id_type=MESH,
        )

    @pl.when(has_prev)
    def _():
        head_copy(prev_device).start()

    def fold(k, scale):
        loads[1 + k].wait()
        product = dot(wsub[...], watt[k])
        center = jnp.mean(wsub[pl.ds(0, stacked_width), :].astype(F32), axis=-1, keepdims=True)
        centered = product[:stacked_width] - center * product[stacked_width : stacked_width + 1]
        folded[k] = (centered * scale).astype(BF16)

    loads[0].wait()
    fold(0, 1.0 / math.sqrt(HD))

    @pl.when(has_next)
    def _():
        head_copy(next_device).wait_recv()

    pieces = [rows[pl.ds(j, own, stride=stride), :] for j in range(stride + 2)]
    frames = []
    for j in range(SUB):
        window = jnp.concatenate(pieces[j : j + WIN // LANES], axis=1)
        shift = (HOP - LANES) * j
        frames.append(pltpu.roll(window, WIN - shift, 1) if shift else window)
    spectrum = wide_dot(jnp.concatenate(frames, axis=0), table_ref)
    power = jnp.square(spectrum[:, :BINS]) + jnp.square(spectrum[:, BINS:])
    mel = jnp.log(wide_dot(power, bank_ref) + 1e-06).astype(BF16)
    stacked = jnp.concatenate([mel[j * own : (j + 1) * own] for j in range(SUB)], axis=1)
    mapped = dot(stacked, wsub[pl.ds(0, stacked_width), :]).astype(BF16)
    features[...] = mapped
    shifted = mapped.astype(F32)
    shifted = shifted - jnp.mean(shifted, axis=-1, keepdims=True)
    spread = jnp.mean(jnp.square(shifted), axis=-1, keepdims=True)
    gathered[here, m] = (stacked.astype(F32) * lax.rsqrt(spread + 1e-05)).astype(BF16)

    def tm_copy(d):
        return pltpu.make_async_remote_copy(
            src_ref=gathered.at[here, m],
            dst_ref=gathered.at[t if absolute else reach - d, m],
            send_sem=tm_send.at[d + reach],
            recv_sem=recv.at[d + reach, 0],
            device_id={"tm": t + d, "mp": m},
            device_id_type=MESH,
        )

    def slot_of(d):
        return t - d if absolute else reach - d

    def mp_copy(d, mask, bit):
        block = gathered.at[slot_of(d), masked_index(m, mask)]
        return pltpu.make_async_remote_copy(
            src_ref=block,
            dst_ref=block,
            send_sem=mp_send.at[d + reach, mask + bit],
            recv_sem=recv.at[d + reach, mask + bit],
            device_id={"tm": t, "mp": flipped(m, bit)},
            device_id_type=MESH,
        )

    def forward(d, mask):
        for bit in reversed(bits):
            if bit < low_bit(mask, n_m):
                mp_copy(d, mask, bit).start()

    def when_sent(d, body):
        pl.when(jnp.logical_and(t + d >= 0, t + d < n_t))(body)

    def when_held(d, body):
        if d == 0:
            body()
        else:
            pl.when(jnp.logical_and(t - d >= 0, t - d < n_t))(body)

    def arrive(d):
        def body():
            tm_copy(d).wait_recv()
            forward(d, 0)

        when_held(d, body)

    def relay(d, mask):
        def body():
            bit = low_bit(mask, n_m)
            mp_copy(d, mask - bit, bit).wait_recv()
            forward(d, mask)

        when_held(d, body)

    def project(slot, asking):
        block = gathered[slot].reshape(shard, stacked_width)
        place = pl.ds(pl.multiple_of(slot * shard, shard), shard)
        if asking:
            query[...] = dot(block, folded[0]).astype(BF16)
        keys[place, :] = dot(block, folded[1]).astype(BF16)
        values[place, :] = dot(block, folded[2]).astype(BF16)

    for d in distances:
        when_sent(d, lambda d=d: tm_copy(d).start())
    forward(0, 0)
    fold(1, 1.0)
    for d in distances[:2]:
        arrive(d)
    fold(2, 1.0)
    for d in distances[2:]:
        arrive(d)
    masks = sorted(range(1, n_m), key=lambda v: -low_bit(v, n_m))
    passing = [mask for mask in masks if mask % 2 == 0]
    ending = [mask for mask in masks if mask % 2]
    for mask in passing:
        relay(0, mask)
    for d in distances[:2]:
        for mask in passing:
            relay(d, mask)
    for mask in ending:
        relay(0, mask)
    project(here, True)
    for d in distances[2:]:
        for mask in passing:
            relay(d, mask)
    for d in distances:
        for mask in ending:
            relay(d, mask)
    for step in range(1, slots):
        project((here + step) % slots, False)

    begin = 0 if absolute else (t - reach) * shard
    loads[4].wait()

    def chunk_rows(mask):
        return pl.ds(pl.multiple_of(masked_index(m, mask) * own, own), own)

    def branch_of(group):
        tall = own * len(group)
        asked = jnp.concatenate([query[chunk_rows(mask), :] for mask in group], axis=0)
        first = jnp.concatenate([bounds[0, chunk_rows(mask), :] for mask in group], axis=0)[:, :1]
        last = jnp.concatenate([bounds[1, chunk_rows(mask), :] for mask in group], axis=0)[:, :1]
        position = lax.broadcasted_iota(jnp.int32, (tall, count), 1) + begin
        allowed = jnp.logical_and(position >= first, position < last)
        mixed_heads = []
        for head in range(local // HD):
            cut = slice(head * HD, (head + 1) * HD)
            scores = lax.dot_general(
                asked[:, cut], keys[:, cut], (((1,), (1,)), ((), ())), preferred_element_type=F32
            )
            scores = jnp.where(allowed, scores, -1e30)
            weights = jnp.exp(scores - jnp.max(scores, axis=-1, keepdims=True))
            total = jnp.sum(weights, axis=-1, keepdims=True)
            mixed_heads.append((dot(weights.astype(BF16), values[:, cut]) / total).astype(BF16))
        return dot(jnp.concatenate(mixed_heads, axis=1), wout[...]).astype(BF16)

    slot_index = {}
    for bit in bits:
        for mask in range(n_m):
            if mask % (2 * bit) == 0:
                slot_index[bit, mask] = len(slot_index)

    def part_copy(bit, mask):
        index = slot_index[bit, mask]
        return pltpu.make_async_remote_copy(
            src_ref=parts.at[mask + bit],
            dst_ref=landed.at[index],
            send_sem=part_send.at[index],
            recv_sem=part_recv.at[index],
            device_id={"tm": t, "mp": flipped(m, bit)},
            device_id_type=MESH,
        )

    odd = [mask for mask in range(n_m) if mask % 2][::-1]
    if odd:
        branches = branch_of(odd)
        for place, mask in enumerate(odd):
            parts[mask] = branches[place * own : (place + 1) * own]
            part_copy(1, mask - 1).start()
    total = None
    for mask in [v for v in range(n_m) if v % 2 == 0][::-1]:
        total = branch_of([mask]).astype(F32)
        for bit in bits:
            if mask % (2 * bit) == 0:
                part_copy(bit, mask).wait_recv()
                total = total + landed[slot_index[bit, mask]].astype(F32)
        if mask:
            parts[mask] = total.astype(BF16)
            low = low_bit(mask, n_m)
            part_copy(low, mask - low).start()
    blended = (features[...].astype(F32) + total).astype(BF16)
    outgoing[...] = blended
    normed = (normalize(blended.astype(F32)) * gain_ref[...]).astype(BF16)
    edges[0] = normed[:EDGE]
    edges[1] = normed[own - EDGE :]

    def edge_copy(side):
        return pltpu.make_async_remote_copy(
            src_ref=edges.at[side],
            dst_ref=edges.at[2 + side],
            send_sem=edge_send.at[side],
            recv_sem=edge_recv.at[side],
            device_id=next_device if side else prev_device,
            device_id_type=MESH,
        )

    @pl.when(has_prev)
    def _():
        edge_copy(0).start()

    @pl.when(has_next)
    def _():
        edge_copy(1).start()

    padded[pl.ds(EDGE, own), :] = normed.astype(F32)
    padded[pl.ds(0, EDGE), :] = jnp.zeros((EDGE, width), F32)
    padded[pl.ds(EDGE + own, EDGE), :] = jnp.zeros((EDGE, width), F32)

    @pl.when(has_next)
    def _():
        edge_copy(0).wait_recv()
        padded[pl.ds(EDGE + own, EDGE), :] = edges[2].astype(F32)

    @pl.when(has_prev)
    def _():
        edge_copy(1).wait_recv()
        padded[pl.ds(0, EDGE), :] = edges[3].astype(F32)

    offset = EDGE - KERNEL // 2

    @pl.loop(0, width // LANES)
    def _(chunk):
        cols = pl.ds(pl.multiple_of(chunk * LANES, LANES), LANES)
        taps = taps_ref[:, cols].astype(F32)
        convolved = jnp.zeros((own, LANES), F32)
        for tap in range(KERNEL):
            convolved = convolved + padded[pl.ds(offset + tap, own), cols] * taps[tap : tap + 1]
        gated = convolved / (1.0 + jnp.exp(-convolved))
        out_ref[:, cols] = (outgoing[:, cols].astype(F32) + gated).astype(BF16)

    for d in distances:
        when_sent(d, lambda d=d: tm_copy(d).wait_send())
    for mask in range(1, n_m):
        bit = low_bit(mask, n_m)
        for d in [0] + distances:
            when_held(d, lambda d=d, mask=mask, bit=bit: mp_copy(d, mask - bit, bit).wait_send())
    for bit, mask in slot_index:
        part_copy(bit, mask).wait_send()

    @pl.when(has_prev)
    def _():
        head_copy(prev_device).wait_send()
        edge_copy(0).wait_send()

    @pl.when(has_next)
    def _():
        edge_copy(1).wait_send()


VMEM = pl.BlockSpec(memory_space=pltpu.VMEM)
HBM = pl.BlockSpec(memory_space=pl.ANY)


def shards(
    n_t, n_m, waveform, segment_start, segment_end, w_subsample, w_attention, w_output,
    gain_convolution, w_depthwise,
):
    own = waveform.shape[0] // (SUB * HOP)
    shard = segment_start.shape[0]
    stacked_width, width = w_subsample.shape
    local = w_attention.shape[2]
    reach = min((SEG_MAX - 2) // shard + 1, n_t - 1)
    absolute = 2 * reach + 1 >= n_t
    slots = n_t if absolute else 2 * reach + 1
    lines = own * SUB * HOP // LANES
    audio = waveform.reshape(lines, LANES)
    dma = pltpu.SemaphoreType.DMA
    spans = 2 * reach + 1
    landings = max(n_m - 1, 1)
    return pl.pallas_call(
        functools.partial(block_kernel, n_t, n_m, reach, absolute),
        out_shape=jax.ShapeDtypeStruct((own, width), BF16),
        in_specs=[VMEM] * 7 + [HBM] * 3,
        out_specs=VMEM,
        scratch_shapes=[
            pltpu.VMEM((lines + 8, LANES), F32),
            pltpu.VMEM((slots, n_m, own, stacked_width), BF16),
            pltpu.VMEM((stacked_width + EDGE, width), BF16),
            pltpu.VMEM((3, width, local), BF16),
            pltpu.VMEM((local, width), BF16),
            pltpu.VMEM((3, stacked_width, local), BF16),
            pltpu.VMEM((shard, local), BF16),
            pltpu.VMEM((slots * shard, local), BF16),
            pltpu.VMEM((slots * shard, local), BF16),
            pltpu.VMEM((2, shard, LANES), jnp.int32),
            pltpu.VMEM((own, width), BF16),
            pltpu.VMEM((n_m, own, width), BF16),
            pltpu.VMEM((landings, own, width), BF16),
            pltpu.VMEM((own, width), BF16),
            pltpu.VMEM((4, EDGE, width), BF16),
            pltpu.VMEM((own + 2 * EDGE, width), F32),
            dma((5,)),
            dma((2,)),
            dma((spans,)),
            dma((spans, n_m)),
            dma((spans, n_m)),
            dma((landings,)),
            dma((landings,)),
            dma((2,)),
            dma((2,)),
        ],
        compiler_params=pltpu.CompilerParams(collective_id=0, has_side_effects=True),
        name="block",
    )(
        audio, jnp.asarray(halves(fourier_table())), jnp.asarray(halves(mel_bank())),
        segment_start.reshape(1, shard), segment_end.reshape(1, shard), gain_convolution.reshape(1, width),
        w_depthwise, w_subsample, w_attention, w_output,
    )


def solution(mesh):
    placed = (
        P(("groups", "tm", "mp")),
        P(("groups", "tm")),
        P(("groups", "tm")),
        P(),
        P(None, None, "mp"),
        P("mp", None),
        P(),
        P(),
    )
    return jax.shard_map(
        functools.partial(shards, mesh.shape["tm"], mesh.shape["mp"]),
        mesh=mesh,
        in_specs=placed,
        out_specs=P(("groups", "tm", "mp"), None),
        check_vma=False,
    )
```

```python
import functools
import math

import jax
import jax.numpy as jnp
import numpy as np
from jax import lax
from jax.experimental import pallas as pl
from jax.experimental.pallas import tpu as pltpu
from jax.sharding import PartitionSpec as P

HD = 64
NMEL = 128
NFFT = 400
HOP = 160
BINS = 256
SUB = 4
KERNEL = 31
SEG_MAX = 750
LANES = 128
WIN = 512
EDGE = 16
MESH = pl.DeviceIdType.MESH
F32 = jnp.float32
BF16 = jnp.bfloat16


def fourier_table():
    sample_index = np.arange(NFFT)[:, None]
    bin_index = np.arange(BINS)[None, :]
    angle = (sample_index * bin_index % NFFT) * (2.0 * math.pi / NFFT)
    window = 0.5 - 0.5 * np.cos(np.arange(NFFT) * (2.0 * math.pi / NFFT))
    kept = bin_index <= NFFT // 2
    cosine = np.where(kept, np.cos(angle), 0.0) * window[:, None]
    sine = np.where(kept, -np.sin(angle), 0.0) * window[:, None]
    table = np.concatenate([cosine, sine], axis=1)
    return np.concatenate([table, np.zeros((WIN - NFFT, 2 * BINS))], axis=0)


def mel_bank():
    mel_top = 2595.0 * math.log10(1.0 + 8000.0 / 700.0)
    points = np.arange(NMEL + 2) * (mel_top / (NMEL + 1))
    edges = 700.0 * (np.power(10.0, points / 2595.0) - 1.0) * (NFFT / 16000.0)
    centers = edges[1:-1]
    widths = np.maximum(edges[2:] - edges[1:-1], 1.0)
    bins = np.arange(BINS)[:, None]
    triangle = np.maximum(0.0, 1.0 - np.abs(bins - centers[None, :]) / widths[None, :])
    return np.where(bins <= NFFT // 2, triangle, 0.0)


def halves(values):
    values = values.astype(np.float32)
    high = values.astype(BF16)
    low = (values - high.astype(np.float32)).astype(BF16)
    return np.stack([high, low])


def split(values):
    high = values.astype(BF16)
    return high, (values - high.astype(F32)).astype(BF16)


def wide_dot(values, table):
    high, low = split(values)
    dot = functools.partial(jnp.dot, preferred_element_type=F32)
    return dot(high, table[0]) + (dot(high, table[1]) + dot(low, table[0]))


def flipped(index, bit):
    return index + bit - 2 * bit * ((index // bit) % 2)


def masked_index(index, mask):
    bit = 1
    while bit <= mask:
        if mask & bit:
            index = flipped(index, bit)
        bit *= 2
    return index


def bits_of(count):
    bits = []
    bit = 1
    while bit < count:
        bits.append(bit)
        bit *= 2
    return bits


def low_bit(mask, count):
    return mask & -mask if mask else count


def normalize(values):
    center = jnp.mean(values, axis=-1, keepdims=True)
    shifted = values - center
    spread = jnp.mean(jnp.square(shifted), axis=-1, keepdims=True)
    return shifted * lax.rsqrt(spread + 1e-05)


def beside(t, m, n_t, n_m, step):
    flat = t * n_m + m + step
    return {"tm": flat // n_m, "mp": flat % n_m}


def signal(sem, device):
    pl.semaphore_signal(sem, inc=1, device_id=device, device_id_type=MESH)


def block_kernel(
    n_t, n_m, reach, absolute, audio_ref, table_ref, bank_ref, start_ref, finish_ref, gain_ref, taps_ref,
    wsub_hbm, watt_hbm, wout_hbm, out_ref,
    rows, gathered, wsub, watt, wout, folded, query, keys, values, bounds, features, parts, landed, outgoing,
    edges, padded, load_sem, head_sem, tm_send, mp_send, recv, part_send, part_recv, edge_send, edge_recv,
):
    t = lax.axis_index("tm")
    m = lax.axis_index("mp")
    slots, _, own, stacked_width = gathered.shape
    shard = n_m * own
    width = out_ref.shape[1]
    local = watt.shape[2]
    count = slots * shard
    stride = SUB * HOP // LANES
    flat = t * n_m + m
    has_prev = flat > 0
    has_next = flat < n_t * n_m - 1
    bits = bits_of(n_m)
    distances = []
    for d in range(1, reach + 1):
        distances += [d, -d]
    dot = functools.partial(jnp.dot, preferred_element_type=F32)
    here = t if absolute else reach
    prev_device = beside(t, m, n_t, n_m, -1)
    next_device = beside(t, m, n_t, n_m, 1)

    loads = [pltpu.make_async_copy(wsub_hbm, wsub.at[pl.ds(0, stacked_width)], load_sem.at[0])]
    for k in range(3):
        loads.append(pltpu.make_async_copy(watt_hbm.at[k], watt.at[k], load_sem.at[1 + k]))
    loads.append(pltpu.make_async_copy(wout_hbm, wout, load_sem.at[4]))
    for load in loads:
        load.start()

    rows[pl.ds(0, own * stride), :] = audio_ref[...]
    rows[pl.ds(own * stride, 8), :] = jnp.zeros((8, LANES), F32)
    if not absolute:
        gathered[...] = jnp.zeros_like(gathered)
    barrier = pltpu.get_barrier_semaphore()
    peers = len(bits) + has_prev.astype(jnp.int32) + has_next.astype(jnp.int32)
    for d in distances:
        inside = jnp.logical_and(t + d >= 0, t + d < n_t)
        peers = peers + inside.astype(jnp.int32)

        @pl.when(inside)
        def _(d=d):
            signal(barrier, {"tm": t + d, "mp": m})

    for bit in bits:
        signal(barrier, {"tm": t, "mp": flipped(m, bit)})

    @pl.when(has_prev)
    def _():
        signal(barrier, prev_device)

    @pl.when(has_next)
    def _():
        signal(barrier, next_device)

    for index, ref in enumerate((start_ref, finish_ref)):
        wide = jnp.broadcast_to(ref[...].astype(F32), (LANES, shard))
        bounds[index] = jnp.transpose(wide).astype(jnp.int32)
    wsub[pl.ds(stacked_width, EDGE), :] = jnp.ones((EDGE, width), BF16)
    pl.semaphore_wait(barrier, peers)

    def head_copy(device):
        return pltpu.make_async_remote_copy(
            src_ref=audio_ref.at[pl.ds(0, 8)],
            dst_ref=rows.at[pl.ds(own * stride, 8)],
            send_sem=head_sem.at[0],
            recv_sem=head_sem.at[1],
            device_id=device,
            device_id_type=MESH,
        )

    @pl.when(has_prev)
    def _():
        head_copy(prev_device).start()

    def fold(k, scale):
        loads[1 + k].wait()
        product = dot(wsub[...], watt[k])
        center = jnp.mean(wsub[pl.ds(0, stacked_width), :].astype(F32), axis=-1, keepdims=True)
        centered = product[:stacked_width] - center * product[stacked_width : stacked_width + 1]
        folded[k] = (centered * scale).astype(BF16)

    loads[0].wait()
    fold(0, 1.0 / math.sqrt(HD))

    @pl.when(has_next)
    def _():
        head_copy(next_device).wait_recv()

    pieces = [rows[pl.ds(j, own, stride=stride), :] for j in range(stride + 2)]
    frames = []
    for j in range(SUB):
        window = jnp.concatenate(pieces[j : j + WIN // LANES], axis=1)
        shift = (HOP - LANES) * j
        frames.append(pltpu.roll(window, WIN - shift, 1) if shift else window)
    spectrum = wide_dot(jnp.concatenate(frames, axis=0), table_ref)
    power = jnp.square(spectrum[:, :BINS]) + jnp.square(spectrum[:, BINS:])
    mel = jnp.log(wide_dot(power, bank_ref) + 1e-06).astype(BF16)
    stacked = jnp.concatenate([mel[j * own : (j + 1) * own] for j in range(SUB)], axis=1)
    mapped = dot(stacked, wsub[pl.ds(0, stacked_width), :]).astype(BF16)
    features[...] = mapped
    shifted = mapped.astype(F32)
    shifted = shifted - jnp.mean(shifted, axis=-1, keepdims=True)
    spread = jnp.mean(jnp.square(shifted), axis=-1, keepdims=True)
    gathered[here, m] = (stacked.astype(F32) * lax.rsqrt(spread + 1e-05)).astype(BF16)

    def tm_copy(d):
        return pltpu.make_async_remote_copy(
            src_ref=gathered.at[here, m],
            dst_ref=gathered.at[t if absolute else reach - d, m],
            send_sem=tm_send.at[d + reach],
            recv_sem=recv.at[d + reach, 0],
            device_id={"tm": t + d, "mp": m},
            device_id_type=MESH,
        )

    def slot_of(d):
        return t - d if absolute else reach - d

    def mp_copy(d, mask, bit):
        block = gathered.at[slot_of(d), masked_index(m, mask)]
        return pltpu.make_async_remote_copy(
            src_ref=block,
            dst_ref=block,
            send_sem=mp_send.at[d + reach, mask + bit],
            recv_sem=recv.at[d + reach, mask + bit],
            device_id={"tm": t, "mp": flipped(m, bit)},
            device_id_type=MESH,
        )

    def forward(d, mask):
        for bit in reversed(bits):
            if bit < low_bit(mask, n_m):
                mp_copy(d, mask, bit).start()

    def when_sent(d, body):
        pl.when(jnp.logical_and(t + d >= 0, t + d < n_t))(body)

    def when_held(d, body):
        if d == 0:
            body()
        else:
            pl.when(jnp.logical_and(t - d >= 0, t - d < n_t))(body)

    def arrive(d):
        def body():
            tm_copy(d).wait_recv()
            forward(d, 0)

        when_held(d, body)

    def relay(d, mask):
        def body():
            bit = low_bit(mask, n_m)
            mp_copy(d, mask - bit, bit).wait_recv()
            forward(d, mask)

        when_held(d, body)

    def project(slot, asking):
        block = gathered[slot].reshape(shard, stacked_width)
        place = pl.ds(pl.multiple_of(slot * shard, shard), shard)
        if asking:
            query[...] = dot(block, folded[0]).astype(BF16)
        keys[place, :] = dot(block, folded[1]).astype(BF16)
        values[place, :] = dot(block, folded[2]).astype(BF16)

    for d in distances[::-1]:
        when_sent(d, lambda d=d: tm_copy(d).start())
    forward(0, 0)
    fold(1, 1.0)
    for d in distances[:2]:
        arrive(d)
    fold(2, 1.0)
    for d in distances[2:]:
        arrive(d)
    masks = sorted(range(1, n_m), key=lambda v: -low_bit(v, n_m))
    passing = [mask for mask in masks if mask % 2 == 0]
    ending = [mask for mask in masks if mask % 2]
    for mask in passing:
        relay(0, mask)
    for d in distances[:2]:
        for mask in passing:
            relay(d, mask)
    for mask in ending:
        relay(0, mask)
    project(here, True)
    for d in distances[2:]:
        for mask in passing:
            relay(d, mask)
    for d in distances:
        for mask in ending:
            relay(d, mask)
    for step in range(1, slots):
        project((here + step) % slots, False)

    begin = 0 if absolute else (t - reach) * shard
    loads[4].wait()

    def chunk_rows(mask):
        return pl.ds(pl.multiple_of(masked_index(m, mask) * own, own), own)

    def branch_of(group):
        tall = own * len(group)
        asked = jnp.concatenate([query[chunk_rows(mask), :] for mask in group], axis=0)
        first = jnp.concatenate([bounds[0, chunk_rows(mask), :] for mask in group], axis=0)[:, :1]
        last = jnp.concatenate([bounds[1, chunk_rows(mask), :] for mask in group], axis=0)[:, :1]
        position = lax.broadcasted_iota(jnp.int32, (tall, count), 1) + begin
        allowed = jnp.logical_and(position >= first, position < last)
        mixed_heads = []
        for head in range(local // HD):
            cut = slice(head * HD, (head + 1) * HD)
            scores = lax.dot_general(
                asked[:, cut], keys[:, cut], (((1,), (1,)), ((), ())), preferred_element_type=F32
            )
            scores = jnp.where(allowed, scores, -1e30)
            weights = jnp.exp(scores - jnp.max(scores, axis=-1, keepdims=True))
            total = jnp.sum(weights, axis=-1, keepdims=True)
            mixed_heads.append((dot(weights.astype(BF16), values[:, cut]) / total).astype(BF16))
        return dot(jnp.concatenate(mixed_heads, axis=1), wout[...]).astype(BF16)

    slot_index = {}
    for bit in bits:
        for mask in range(n_m):
            if mask % (2 * bit) == 0:
                slot_index[bit, mask] = len(slot_index)

    def part_copy(bit, mask):
        index = slot_index[bit, mask]
        return pltpu.make_async_remote_copy(
            src_ref=parts.at[mask + bit],
            dst_ref=landed.at[index],
            send_sem=part_send.at[index],
            recv_sem=part_recv.at[index],
            device_id={"tm": t, "mp": flipped(m, bit)},
            device_id_type=MESH,
        )

    groups = [[mask] for mask in range(n_m)][:1:-1] + [list(range(min(n_m, 2)))[::-1]]
    total = None
    for group in groups:
        branches = branch_of(group)
        for place, mask in enumerate(group):
            part = branches[place * own : (place + 1) * own]
            if mask % 2:
                parts[mask] = part
                part_copy(1, mask - 1).start()
                continue
            total = part.astype(F32)
            for bit in bits:
                if mask % (2 * bit) == 0:
                    part_copy(bit, mask).wait_recv()
                    total = total + landed[slot_index[bit, mask]].astype(F32)
            if mask:
                parts[mask] = total.astype(BF16)
                low = low_bit(mask, n_m)
                part_copy(low, mask - low).start()
    blended = (features[...].astype(F32) + total).astype(BF16)
    outgoing[...] = blended
    normed = (normalize(blended.astype(F32)) * gain_ref[...][None, :]).astype(BF16)
    edges[0] = normed[:EDGE]
    edges[1] = normed[own - EDGE :]

    def edge_copy(side):
        return pltpu.make_async_remote_copy(
            src_ref=edges.at[side],
            dst_ref=edges.at[2 + side],
            send_sem=edge_send.at[side],
            recv_sem=edge_recv.at[side],
            device_id=next_device if side else prev_device,
            device_id_type=MESH,
        )

    @pl.when(has_prev)
    def _():
        edge_copy(0).start()

    @pl.when(has_next)
    def _():
        edge_copy(1).start()

    padded[pl.ds(EDGE, own), :] = normed.astype(F32)
    padded[pl.ds(0, EDGE), :] = jnp.zeros((EDGE, width), F32)
    padded[pl.ds(EDGE + own, EDGE), :] = jnp.zeros((EDGE, width), F32)

    @pl.when(has_next)
    def _():
        edge_copy(0).wait_recv()
        padded[pl.ds(EDGE + own, EDGE), :] = edges[2].astype(F32)

    @pl.when(has_prev)
    def _():
        edge_copy(1).wait_recv()
        padded[pl.ds(0, EDGE), :] = edges[3].astype(F32)

    offset = EDGE - KERNEL // 2

    @pl.loop(0, width // LANES)
    def _(chunk):
        cols = pl.ds(pl.multiple_of(chunk * LANES, LANES), LANES)
        taps = taps_ref[:, cols].astype(F32)
        convolved = jnp.zeros((own, LANES), F32)
        for tap in range(KERNEL):
            convolved = convolved + padded[pl.ds(offset + tap, own), cols] * taps[tap : tap + 1]
        gated = convolved / (1.0 + jnp.exp(-convolved))
        out_ref[:, cols] = (outgoing[:, cols].astype(F32) + gated).astype(BF16)

    for d in distances:
        when_sent(d, lambda d=d: tm_copy(d).wait_send())
    for mask in range(1, n_m):
        bit = low_bit(mask, n_m)
        for d in [0] + distances:
            when_held(d, lambda d=d, mask=mask, bit=bit: mp_copy(d, mask - bit, bit).wait_send())
    for bit, mask in slot_index:
        part_copy(bit, mask).wait_send()

    @pl.when(has_prev)
    def _():
        head_copy(prev_device).wait_send()
        edge_copy(0).wait_send()

    @pl.when(has_next)
    def _():
        edge_copy(1).wait_send()


VMEM = pl.BlockSpec(memory_space=pltpu.VMEM)
HBM = pl.BlockSpec(memory_space=pl.ANY)


def shards(
    n_t, n_m, waveform, segment_start, segment_end, w_subsample, w_attention, w_output,
    gain_convolution, w_depthwise,
):
    own = waveform.shape[0] // (SUB * HOP)
    shard = segment_start.shape[0]
    stacked_width, width = w_subsample.shape
    local = w_attention.shape[2]
    reach = min((SEG_MAX - 2) // shard + 1, n_t - 1)
    absolute = 2 * reach + 1 >= n_t
    slots = n_t if absolute else 2 * reach + 1
    lines = own * SUB * HOP // LANES
    audio = waveform.reshape(lines, LANES)
    dma = pltpu.SemaphoreType.DMA
    spans = 2 * reach + 1
    landings = max(n_m - 1, 1)
    return pl.pallas_call(
        functools.partial(block_kernel, n_t, n_m, reach, absolute),
        out_shape=jax.ShapeDtypeStruct((own, width), BF16),
        in_specs=[VMEM] * 7 + [HBM] * 3,
        out_specs=VMEM,
        scratch_shapes=[
            pltpu.VMEM((lines + 8, LANES), F32),
            pltpu.VMEM((slots, n_m, own, stacked_width), BF16),
            pltpu.VMEM((stacked_width + EDGE, width), BF16),
            pltpu.VMEM((3, width, local), BF16),
            pltpu.VMEM((local, width), BF16),
            pltpu.VMEM((3, stacked_width, local), BF16),
            pltpu.VMEM((shard, local), BF16),
            pltpu.VMEM((slots * shard, local), BF16),
            pltpu.VMEM((slots * shard, local), BF16),
            pltpu.VMEM((2, shard, LANES), jnp.int32),
            pltpu.VMEM((own, width), BF16),
            pltpu.VMEM((n_m, own, width), BF16),
            pltpu.VMEM((landings, own, width), BF16),
            pltpu.VMEM((own, width), BF16),
            pltpu.VMEM((4, EDGE, width), BF16),
            pltpu.VMEM((own + 2 * EDGE, width), F32),
            dma((5,)),
            dma((2,)),
            dma((spans,)),
            dma((spans, n_m)),
            dma((spans, n_m)),
            dma((landings,)),
            dma((landings,)),
            dma((2,)),
            dma((2,)),
        ],
        compiler_params=pltpu.CompilerParams(collective_id=0, has_side_effects=True),
        name="block",
    )(
        audio, jnp.asarray(halves(fourier_table())), jnp.asarray(halves(mel_bank())),
        segment_start.reshape(1, shard), segment_end.reshape(1, shard), gain_convolution,
        w_depthwise, w_subsample, w_attention, w_output,
    )


def solution(mesh):
    placed = (
        P(("groups", "tm", "mp")),
        P(("groups", "tm")),
        P(("groups", "tm")),
        P(),
        P(None, None, "mp"),
        P("mp", None),
        P(),
        P(),
    )
    return jax.shard_map(
        functools.partial(shards, mesh.shape["tm"], mesh.shape["mp"]),
        mesh=mesh,
        in_specs=placed,
        out_specs=P(("groups", "tm", "mp"), None),
        check_vma=False,
    )
```
